512 devices in a mesh: prow: 16 (over z_lo, x, core), pcol: 32 (over z_hi, y).
Axes of the slice: x: 4, y: 8, z: 8 (z_hi: 4, z_lo: 2; z = z_hi * 2 + z_lo), core: 2. Of those that a mesh axis runs over, the one named last changes fastest.
Arguments:
- trailing: float32 [8192, 8192], P('prow', 'pcol'), may hold values from -6 to 6
- panels: float32 [8192, 1024], P('prow', 'pcol'), may hold values from -0.09375 to 0.09375
- diag_inv: float32 [4, 256, 256], replicated, may hold values from -6 to 6
- ancestors: int32 [4, 16], replicated, may hold values from 0 to 31, as said below
- owner_map: int32 [32], replicated, may hold values from 0 to 31, each once
Outputs:
- inv_panel: float32 [8192, 1024], P(('prow', 'pcol'))
- inv_upper: float32 [1024, 8192], P('pcol', 'prow')
- inv_diag: float32 [4, 256, 256], replicated
The draws below stay inside these ranges and needn't reach their ends.
Inputs may be any that keep to these rules, and one draw needn't show every extreme that they name: `ancestors`: each row names 16 distinct blocks; every block is named by exactly two siblings.
All inputs are finite; a program needn't handle non-finite values.
Results may differ from the reference program's by a relative error of at most 0.000071.
Values sent between devices are 32-bit elements; how exact they have to be, the bound alone decides.
No kernel may reach another device: no remote copies, remote signals or barrier semaphores. Data moves between devices by JAX's collectives and lax.ppermute only.
A program may use at most 64 MiB of HBM per device.

```python
import jax
import jax.numpy as jnp
from jax import lax

NB = 256
SIBS = 4
NBLK = 32
ROWS = 8192
ANC_SET = 16
PANEL = 1024


def draw_ancestors(key, part):
    base = jax.random.permutation(jax.random.fold_in(key, 17), NBLK).astype(jnp.int32)
    offsets = jnp.arange(ANC_SET, dtype=jnp.int32)
    starts = jnp.arange(SIBS, dtype=jnp.int32) * (NBLK // SIBS)
    places = (starts[:, None] + offsets[None, :]) % NBLK
    return base[places].astype(jnp.int32)


def steps_of(rng, extent, cuts, least, high):
    gain, own = 1.0, jax.random.fold_in(rng, 6)
    for axis_at, blocks in cuts:
        steps = jnp.exp(jax.random.uniform(jax.random.fold_in(own, axis_at), (blocks,), jnp.float32, least / len(cuts), high / len(cuts)))
        gain = gain * jnp.repeat(steps, extent[axis_at] // blocks).reshape([-1 if axis == axis_at else 1 for axis in range(len(extent))])
    return gain


def scatter_about(stream_key, extent, width, reach, pieces=(), kind=jnp.bfloat16):
    loudness = steps_of(stream_key, extent, pieces, -0.22, 0.18) if pieces else 1.0
    result = jax.random.normal(stream_key, extent, jnp.float32) * width * loudness
    return jnp.minimum(jnp.maximum(result, -reach), reach).astype(kind)


def setup_inputs(seed: int = 0) -> dict:
    key_list = jax.random.split(jax.random.key(seed), 6)
    return {
        "trailing": scatter_about(key_list[0], (ROWS, ROWS), 1.0, 6.0, ((0, 16), (1, 32)), jnp.float32),
        "panels": scatter_about(key_list[1], (ROWS, PANEL), (NB * NBLK // 2) ** -0.5, 0.09375, ((0, 16), (1, 32)), jnp.float32),
        "diag_inv": scatter_about(key_list[2], (SIBS, NB, NB), 1.0, 6.0, (), jnp.float32),
        "ancestors": draw_ancestors(jax.random.fold_in(key_list[5], 71), 0),
        "owner_map": jax.random.permutation(key_list[4], NBLK).astype(jnp.int32),
    }


def reference(trailing, panels, diag_inv, ancestors, owner_map):
    nblk = owner_map.shape[0]
    slots = owner_map[ancestors]
    member = jnp.any(slots[:, :, None] == jnp.arange(nblk, dtype=jnp.int32)[None, None, :], axis=1).astype(jnp.float32)
    mask = jnp.repeat(jnp.repeat(member.T, NB, axis=0), NB, axis=1)
    masked = panels * mask
    product = jnp.dot(trailing, masked, precision=lax.Precision.HIGHEST, preferred_element_type=jnp.float32)
    inv_panel = -product * mask
    inv_upper = inv_panel.T
    term = jnp.einsum("rjn,rjm->jnm", masked.reshape(-1, SIBS, NB), inv_panel.reshape(-1, SIBS, NB), precision=lax.Precision.HIGHEST)
    inv_diag = diag_inv - term
    return inv_panel, inv_upper, inv_diag
```

```python
import jax
import jax.numpy as jnp
import numpy as np
from jax import lax
from jax.sharding import Mesh, PartitionSpec as P

NB = 256
SIBS = 4
PROW = ("zlo", "x", "core")
PCOL = ("zhi", "y")
HIGH = lax.Precision.HIGH
HIGHEST = lax.Precision.HIGHEST


def exchange(array, axes):
    return lax.all_to_all(array, axes, 0, 0, tiled=True)


def pick(first, last, t):
    return first if t == 0 else last


def shards(trailing, panels, diag_inv, ancestors, owner_map):
    row = lax.axis_index(PROW)
    col = lax.axis_index(PCOL)
    nrow, ncol = 16, 32
    nblk = owner_map.shape[0]

    blocks = jnp.stack([col, 2 * row, 2 * row + 1, 2 * row + col // 16])
    number = jnp.sum(
        jnp.where(owner_map[None, :] == blocks[:, None], jnp.arange(nblk)[None, :], 0), axis=1
    )
    named = jnp.any(ancestors[None, :, :] == number[:, None, None], axis=2)
    sibling = jnp.arange(SIBS, dtype=jnp.int32)[None, :]
    first = jnp.min(jnp.where(named, sibling, SIBS), axis=1)
    last = jnp.max(jnp.where(named, sibling, -1), axis=1)

    factor_t = panels.T
    sib_rows = exchange(jnp.broadcast_to(factor_t[None], (8, 32, 512)), "y").reshape(256, 512)

    spread = exchange(factor_t.reshape(nrow, 2, 512), PROW)
    spread = spread.reshape(nrow, 2, 2, NB).transpose(0, 2, 1, 3).reshape(ncol, 2, NB)
    spread = exchange(spread, PCOL).reshape(SIBS, 16, NB)
    active = jnp.concatenate(
        [
            lax.dynamic_index_in_dim(spread, first[0], 0),
            lax.dynamic_index_in_dim(spread, last[0], 0),
        ],
        axis=0,
    )
    active = exchange(jnp.broadcast_to(active.reshape(1, 32, NB), (nrow, 32, NB)), PROW)
    active = active.reshape(nrow, 2, 16, NB)

    mine = (first[0], last[0])
    sides = []
    for h in range(2):
        for t in range(2):
            want = pick(first[1 + h], last[1 + h], t)
            sides.append(
                jnp.where(mine[0] == want, active[:, 0], 0.0)
                + jnp.where(mine[1] == want, active[:, 1], 0.0)
            )
    sides = jnp.stack(sides).reshape(2, 512, NB)
    product = lax.dot_general(
        trailing.reshape(2, NB, NB),
        sides,
        (((2,), (2,)), ((0,), (0,))),
        precision=HIGH,
        preferred_element_type=jnp.float32,
    )
    pieces = exchange(product.reshape(ncol, 16, 512), PCOL)
    reduced = jnp.sum(pieces, axis=0)

    source = jnp.arange(512, dtype=jnp.int32)
    slot = source // 256
    within = source % 16 // 2 * 32 + source % 256 // 16 * 2 + source % 2
    place = jnp.where(slot == 0, first[3], last[3]) * NB + within
    expand = jnp.where(place[:, None] == jnp.arange(1024, dtype=jnp.int32)[None, :], -1.0, 0.0)
    inv_panel = jnp.dot(reduced, expand, precision=HIGHEST, preferred_element_type=jnp.float32)

    upper = exchange(inv_panel.reshape(16, ncol, 32).transpose(1, 2, 0), PCOL)
    inv_upper = upper.transpose(1, 0, 2).reshape(32, 512)

    term = lax.dot_general(
        sib_rows,
        inv_upper,
        (((1,), (1,)), ((), ())),
        precision=HIGH,
        preferred_element_type=jnp.float32,
    )
    term = jnp.sum(exchange(term.reshape(nrow, 16, 32), PROW), axis=0)
    term = exchange(jnp.broadcast_to(term[None], (ncol, 16, 32)), PCOL)
    term = term.reshape(SIBS, 8, 16, 32).transpose(0, 2, 1, 3).reshape(64, NB)
    term = exchange(jnp.broadcast_to(term[None], (nrow, 64, NB)), PROW)
    term = term.reshape(nrow, SIBS, 16, NB).transpose(1, 0, 2, 3).reshape(SIBS, NB, NB)
    inv_diag = diag_inv - term
    return (inv_panel, inv_upper, inv_diag)


def solution(mesh):
    grid = Mesh(mesh.devices.reshape(2, 4, 2, 4, 8), PROW + PCOL)
    placed = (P(PROW, PCOL), P(PROW, PCOL), P(), P(), P())
    return jax.shard_map(
        shards,
        mesh=grid,
        in_specs=placed,
        out_specs=(P(PROW + PCOL, None), P(PCOL, PROW), P()),
        check_vma=False,
    )
```

```python
import jax
import jax.numpy as jnp
from jax import lax
from jax.sharding import Mesh, PartitionSpec as P

NB = 256
SIBS = 4
PROW = ("zlo", "x", "core")
PCOL = ("zhi", "yhi", "ylo")
NROW = 16
NCOL = 32
HIGH = lax.Precision.HIGH


def exchange(array, axes):
    return lax.all_to_all(array, axes, 0, 0, tiled=True)


def to_all(array, count):
    return jnp.broadcast_to(array[None], (count,) + array.shape)


def column_of_block():
    pairs = []
    for p in range(NROW):
        for s in range(SIBS):
            for c in range(8):
                source = p * NCOL + s * 8 + c
                target = (c * 2 + s // 2) * NCOL + 2 * p + s % 2
                pairs.append((source, target))
    return pairs


def shards(trailing, panels, diag_inv, ancestors, owner_map):
    row = lax.axis_index(PROW)
    col = lax.axis_index(PCOL)
    core = lax.axis_index("core")
    nblk = owner_map.shape[0]

    factor_t = panels.T
    moved = lax.ppermute(factor_t, PROW + PCOL, column_of_block())

    blocks = jnp.stack([col, 2 * row, 2 * row + 1, 2 * row + col // 16])
    number = jnp.sum(
        jnp.where(owner_map[None, :] == blocks[:, None], jnp.arange(nblk)[None, :], 0), axis=1
    )
    named = jnp.any(ancestors[None, :, :] == number[:, None, None], axis=2)
    sibling = jnp.arange(SIBS, dtype=jnp.int32)[None, :]
    first = jnp.min(jnp.where(named, sibling, SIBS), axis=1)
    last = jnp.max(jnp.where(named, sibling, -1), axis=1)

    halves = moved.reshape(32, 2, NB).transpose(1, 0, 2)
    whole = exchange(to_all(halves, NROW).reshape(NCOL, 32, NB), PROW + ("ylo",))
    whole = whole.reshape(8, SIBS, 32, NB)

    sides = []
    for h in range(2):
        for want in (first[1 + h], last[1 + h]):
            side = lax.dynamic_index_in_dim(whole, want, 1)
            held = (first[0] == want) | (last[0] == want)
            sides.append(jnp.where(held, side, 0.0))
    sides = jnp.stack(sides).reshape(2, 512, NB)
    product = lax.dot_general(
        trailing.reshape(2, NB, NB),
        sides,
        (((2,), (2,)), ((0,), (0,))),
        precision=HIGH,
        preferred_element_type=jnp.float32,
    )
    pieces = exchange(product.reshape(NCOL, 16, 512), PCOL)
    reduced = jnp.sum(pieces, axis=0).reshape(16, 2, NB)

    result = jnp.stack(
        [
            jnp.where(
                first[3] == s, -reduced[:, 0], jnp.where(last[3] == s, -reduced[:, 1], 0.0)
            )
            for s in range(SIBS)
        ]
    )
    inv_panel = result.transpose(1, 0, 2).reshape(16, SIBS * NB)

    upper = jnp.broadcast_to(result[:, None], (SIBS, 8, 16, NB)).reshape(NCOL, 16, NB)
    upper = exchange(upper, PCOL).reshape(512, NB)
    part = lax.dynamic_slice_in_dim(upper, col % 8 * 32, 32, 1)
    inv_upper = part.T

    term = jnp.dot(factor_t, upper, precision=HIGH, preferred_element_type=jnp.float32)
    term = exchange(to_all(term.reshape(2, 16, NB), 8).reshape(NROW, 16, NB), PROW)
    term = jnp.sum(term, axis=0)
    mine = exchange(to_all(term, NCOL), PCOL)
    other = lax.ppermute(mine, "core", [(0, 1), (1, 0)])
    low = jnp.where(core == 0, mine, other).reshape(SIBS, 8, 1, 16, NB)
    high = jnp.where(core == 0, other, mine).reshape(SIBS, 8, 1, 16, NB)
    term = jnp.concatenate([low, high], axis=2).reshape(SIBS, NB, NB)
    inv_diag = diag_inv - term
    return (inv_panel, inv_upper, inv_diag)


def solution(mesh):
    grid = Mesh(mesh.devices.reshape(2, 4, 2, 4, 4, 2), PROW + PCOL)
    placed = (P(PROW, PCOL), P(PROW, PCOL), P(), P(), P())
    return jax.shard_map(
        shards,
        mesh=grid,
        in_specs=placed,
        out_specs=(P(PROW + PCOL, None), P(PCOL, PROW), P()),
        check_vma=False,
    )
```

```python
import jax
import jax.numpy as jnp
from jax import lax
from jax.sharding import Mesh, PartitionSpec as P

NB = 256
SIBS = 4
PROW = ("zlo", "x", "core")
PCOL = ("zhi", "yhi", "ylo")
NROW = 16
NCOL = 32
HIGH = lax.Precision.HIGH


def exchange(array, axes):
    return lax.all_to_all(array, axes, 0, 0, tiled=True)


def to_all(array, count):
    return jnp.broadcast_to(array[None], (count,) + array.shape)


def column_of_block():
    pairs = []
    for p in range(NROW):
        for s in range(SIBS):
            for c in range(8):
                source = p * NCOL + s * 8 + c
                target = (c * 2 + s // 2) * NCOL + 2 * p + s % 2
                pairs.append((source, target))
    return pairs


def shards(trailing, panels, diag_inv, ancestors, owner_map):
    row = lax.axis_index(PROW)
    col = lax.axis_index(PCOL)
    core = lax.axis_index("core")
    nblk = owner_map.shape[0]

    factor_t = panels.T
    moved = lax.ppermute(factor_t, PROW + PCOL, column_of_block())

    blocks = jnp.stack([col, 2 * row, 2 * row + 1, 2 * row + col // 16])
    number = jnp.sum(
        jnp.where(owner_map[None, :] == blocks[:, None], jnp.arange(nblk)[None, :], 0), axis=1
    )
    named = jnp.any(ancestors[None, :, :] == number[:, None, None], axis=2)
    sibling = jnp.arange(SIBS, dtype=jnp.int32)[None, :]
    first = jnp.min(jnp.where(named, sibling, SIBS), axis=1)
    last = jnp.max(jnp.where(named, sibling, -1), axis=1)

    parts = moved.reshape(2, 16, 2, NB).transpose(0, 2, 1, 3).reshape(SIBS, 16, NB)
    parts = exchange(parts, ("core", "ylo"))
    parts = jnp.concatenate(
        [
            lax.dynamic_index_in_dim(parts, first[0], 0),
            lax.dynamic_index_in_dim(parts, last[0], 0),
        ]
    )
    block = exchange(to_all(parts.reshape(32, NB), NROW), PROW).reshape(NROW, 2, 16, NB)

    sides = []
    for h in range(2):
        for want in (first[1 + h], last[1 + h]):
            sides.append(
                jnp.where(first[0] == want, block[:, 0], 0.0)
                + jnp.where(last[0] == want, block[:, 1], 0.0)
            )
    sides = jnp.stack(sides).reshape(2, 512, NB)
    product = lax.dot_general(
        trailing.reshape(2, NB, NB),
        sides,
        (((2,), (2,)), ((0,), (0,))),
        precision=HIGH,
        preferred_element_type=jnp.float32,
    )
    pieces = exchange(product.reshape(NCOL, 16, 512), PCOL)
    reduced = jnp.sum(pieces, axis=0).reshape(16, 2, NB)

    result = jnp.stack(
        [
            jnp.where(
                first[3] == s, -reduced[:, 0], jnp.where(last[3] == s, -reduced[:, 1], 0.0)
            )
            for s in range(SIBS)
        ]
    )
    inv_panel = result.transpose(1, 0, 2).reshape(16, SIBS * NB)

    upper = jnp.broadcast_to(result[:, None], (SIBS, 8, 16, NB)).reshape(NCOL, 16, NB)
    upper = exchange(upper, PCOL).reshape(512, NB)
    part = lax.dynamic_slice_in_dim(upper, col % 8 * 32, 32, 1)
    inv_upper = part.T

    term = jnp.dot(factor_t, upper, precision=HIGH, preferred_element_type=jnp.float32)
    term = exchange(to_all(term.reshape(2, 16, NB), 8).reshape(NROW, 16, NB), PROW)
    term = jnp.sum(term, axis=0)
    mine = exchange(to_all(term, NCOL), PCOL)
    other = lax.ppermute(mine, "core", [(0, 1), (1, 0)])
    low = jnp.where(core == 0, mine, other).reshape(SIBS, 8, 1, 16, NB)
    high = jnp.where(core == 0, other, mine).reshape(SIBS, 8, 1, 16, NB)
    term = jnp.concatenate([low, high], axis=2).reshape(SIBS, NB, NB)
    inv_diag = diag_inv - term
    return (inv_panel, inv_upper, inv_diag)


def solution(mesh):
    grid = Mesh(mesh.devices.reshape(2, 4, 2, 4, 4, 2), PROW + PCOL)
    placed = (P(PROW, PCOL), P(PROW, PCOL), P(), P(), P())
    return jax.shard_map(
        shards,
        mesh=grid,
        in_specs=placed,
        out_specs=(P(PROW + PCOL, None), P(PCOL, PROW), P()),
        check_vma=False,
    )
```

```python
import jax
import jax.numpy as jnp
from jax import lax
from jax.sharding import Mesh, PartitionSpec as P

NB = 256
SIBS = 4
PROW = ("zlo", "x", "core")
PCOL = ("zhi", "yhi", "ylo")
NROW = 16
NCOL = 32
HIGH = lax.Precision.HIGH


def exchange(array, axes):
    return lax.all_to_all(array, axes, 0, 0, tiled=True)


def to_all(array, count):
    return jnp.broadcast_to(array[None], (count,) + array.shape)


def column_of_block():
    pairs = []
    for p in range(NROW):
        for s in range(SIBS):
            for c in range(8):
                source = p * NCOL + s * 8 + c
                target = (c * 2 + s // 2) * NCOL + 2 * p + s % 2
                pairs.append((source, target))
    return pairs


def shards(trailing, panels, diag_inv, ancestors, owner_map):
    row = lax.axis_index(PROW)
    col = lax.axis_index(PCOL)
    core = lax.axis_index("core")
    nblk = owner_map.shape[0]

    factor_t = panels.T
    moved = lax.ppermute(factor_t, PROW + PCOL, column_of_block())

    blocks = jnp.stack([col, 2 * row, 2 * row + 1, 2 * row + col // 16])
    number = jnp.sum(
        jnp.where(owner_map[None, :] == blocks[:, None], jnp.arange(nblk)[None, :], 0), axis=1
    )
    named = jnp.any(ancestors[None, :, :] == number[:, None, None], axis=2)
    sibling = jnp.arange(SIBS, dtype=jnp.int32)[None, :]
    first = jnp.min(jnp.where(named, sibling, SIBS), axis=1)
    last = jnp.max(jnp.where(named, sibling, -1), axis=1)
    slots = jnp.stack([first, last], axis=1)
    chosen = (slots[0][:, None] == sibling).reshape(8)
    matched = (slots[1:3].reshape(4)[:, None] == slots[0][None, :]).reshape(8)
    placed = (slots[3][:, None] == sibling).reshape(8)
    masks = jnp.concatenate([chosen, matched, placed]).astype(jnp.float32)
    masks = lax.optimization_barrier(jnp.broadcast_to(masks[:, None], (24, NB)))
    chosen = masks[0:8].reshape(2, SIBS, 1, NB)
    matched = masks[8:16].reshape(2, 2, 2, 1, 1, NB)
    placed = masks[16:24].reshape(2, SIBS, 1, NB)

    parts = moved.reshape(2, 16, 2, NB).transpose(0, 2, 1, 3).reshape(SIBS, 16, NB)
    parts = exchange(parts, ("core", "ylo"))
    parts = jnp.sum(chosen * parts[None], axis=1)
    block = exchange(to_all(parts.reshape(32, NB), NROW), PROW).reshape(NROW, 2, 16, NB)

    sides = matched[:, :, 0] * block[None, None, :, 0] + matched[:, :, 1] * block[None, None, :, 1]
    sides = sides.reshape(2, 512, NB)
    product = lax.dot_general(
        trailing.reshape(2, NB, NB),
        sides,
        (((2,), (2,)), ((0,), (0,))),
        precision=HIGH,
        preferred_element_type=jnp.float32,
    )
    pieces = exchange(product.reshape(NCOL, 16, 512), PCOL)
    reduced = jnp.sum(pieces, axis=0).reshape(16, 2, NB)

    result = -(placed[0] * reduced[None, :, 0] + placed[1] * reduced[None, :, 1])
    inv_panel = result.transpose(1, 0, 2).reshape(16, SIBS * NB)

    upper = jnp.broadcast_to(result[:, None], (SIBS, 8, 16, NB)).reshape(NCOL, 16, NB)
    upper = exchange(upper, PCOL).reshape(512, NB)
    part = lax.dynamic_slice_in_dim(upper, col % 8 * 32, 32, 1)
    inv_upper = part.T

    term = jnp.dot(factor_t, upper, precision=HIGH, preferred_element_type=jnp.float32)
    term = exchange(to_all(term.reshape(2, 16, NB), 8).reshape(NROW, 16, NB), PROW)
    term = jnp.sum(term, axis=0)
    mine = exchange(to_all(term, NCOL), PCOL)
    other = lax.ppermute(mine, "core", [(0, 1), (1, 0)])
    low = jnp.where(core == 0, mine, other).reshape(SIBS, 8, 1, 16, NB)
    high = jnp.where(core == 0, other, mine).reshape(SIBS, 8, 1, 16, NB)
    term = jnp.concatenate([low, high], axis=2).reshape(SIBS, NB, NB)
    inv_diag = diag_inv - term
    return (inv_panel, inv_upper, inv_diag)


def solution(mesh):
    grid = Mesh(mesh.devices.reshape(2, 4, 2, 4, 4, 2), PROW + PCOL)
    placed = (P(PROW, PCOL), P(PROW, PCOL), P(), P(), P())
    return jax.shard_map(
        shards,
        mesh=grid,
        in_specs=placed,
        out_specs=(P(PROW + PCOL, None), P(PCOL, PROW), P()),
        check_vma=False,
    )
```

```python
import jax
import jax.numpy as jnp
from jax import lax
from jax.experimental import pallas as pl
from jax.experimental.pallas import tpu as pltpu
from jax.sharding import Mesh, PartitionSpec as P

NB = 256
SIBS = 4
PROW = ("zlo", "x", "core")
PCOL = ("zhi", "yhi", "ylo")
NROW = 16
NCOL = 32
LANES = 128
HIGH = lax.Precision.HIGH


def exchange(array, axes):
    return lax.all_to_all(array, axes, 0, 0, tiled=True)


def to_all(array, count):
    return jnp.broadcast_to(array[None], (count,) + array.shape)


def column_of_block():
    pairs = []
    for p in range(NROW):
        for s in range(SIBS):
            for c in range(8):
                source = p * NCOL + s * 8 + c
                target = (c * 2 + s // 2) * NCOL + 2 * p + s % 2
                pairs.append((source, target))
    return pairs


def assemble_kernel(core_ref, mine_ref, other_ref, diag_ref, out_ref):
    low_is_mine = core_ref[0] == 0
    for half in range(2):
        lanes = pl.ds(half * LANES, LANES)
        for part in range(4):
            for e in range(2):
                mine = mine_ref[half * 4 + part, pl.ds(e * 16, 16), :]
                other = other_ref[half * 4 + part, pl.ds(e * 16, 16), :]
                low = jnp.where(low_is_mine, mine, other)
                high = jnp.where(low_is_mine, other, mine)
                first = (e * 4 + part) * 32
                for rows, term in ((pl.ds(first, 16), low), (pl.ds(first + 16, 16), high)):
                    out_ref[0, rows, lanes] = diag_ref[0, rows, lanes] - term


def assemble(core, mine, other, diag_inv):
    pieces = pl.BlockSpec((8, 32, LANES), lambda s, core_ref: (s, 0, 0))
    block = pl.BlockSpec((1, NB, NB), lambda s, core_ref: (s, 0, 0))
    return pl.pallas_call(
        assemble_kernel,
        grid_spec=pltpu.PrefetchScalarGridSpec(
            num_scalar_prefetch=1,
            grid=(SIBS,),
            in_specs=[pieces, pieces, block],
            out_specs=block,
        ),
        out_shape=jax.ShapeDtypeStruct((SIBS, NB, NB), jnp.float32),
        compiler_params=pltpu.CompilerParams(vmem_limit_bytes=4 * 1024 * 1024),
    )(core, mine, other, diag_inv)


def shards(trailing, panels, diag_inv, ancestors, owner_map):
    row = lax.axis_index(PROW)
    col = lax.axis_index(PCOL)
    nblk = owner_map.shape[0]

    factor_t = panels.T
    moved = lax.ppermute(factor_t, PROW + PCOL, column_of_block())
    across = lax.ppermute(factor_t, "yhi", [(0, 2), (1, 3), (2, 0), (3, 1)])
    right = lax.axis_index("yhi") >= 2
    pair = jnp.concatenate(
        [jnp.where(right, across, factor_t), jnp.where(right, factor_t, across)]
    )

    blocks = jnp.stack([col, 2 * row, 2 * row + 1, 2 * row + col // 16])
    number = jnp.sum(
        jnp.where(owner_map[None, :] == blocks[:, None], jnp.arange(nblk)[None, :], 0), axis=1
    )
    named = jnp.any(ancestors[None, :, :] == number[:, None, None], axis=2)
    sibling = jnp.arange(SIBS, dtype=jnp.int32)[None, :]
    first = jnp.min(jnp.where(named, sibling, SIBS), axis=1)
    last = jnp.max(jnp.where(named, sibling, -1), axis=1)
    slots = jnp.stack([first, last], axis=1)
    chosen = (slots[0][:, None] == sibling).reshape(8)
    matched = (slots[1:3].reshape(4)[:, None] == slots[0][None, :]).reshape(8)
    placed = (slots[3][:, None] == sibling).reshape(8)
    masks = jnp.concatenate([chosen, matched, placed]).astype(jnp.float32)
    masks = lax.optimization_barrier(jnp.broadcast_to(masks[:, None], (24, NB)))
    chosen = masks[0:8].reshape(2, SIBS, 1, NB)
    matched = masks[8:16].reshape(2, 2, 2, 1, 1, NB)
    placed = masks[16:24].reshape(2, SIBS, 1, NB)

    parts = moved.reshape(2, 16, 2, NB).transpose(0, 2, 1, 3).reshape(SIBS, 16, NB)
    parts = exchange(parts, ("core", "ylo"))
    parts = jnp.sum(chosen * parts[None], axis=1)
    block = exchange(to_all(parts.reshape(32, NB), NROW), PROW).reshape(NROW, 2, 16, NB)

    sides = matched[:, :, 0] * block[None, None, :, 0] + matched[:, :, 1] * block[None, None, :, 1]
    sides = sides.reshape(2, 512, NB)
    product = lax.dot_general(
        trailing.reshape(2, NB, NB),
        sides,
        (((2,), (2,)), ((0,), (0,))),
        precision=HIGH,
        preferred_element_type=jnp.float32,
    )
    pieces = exchange(product.reshape(NCOL, 16, 512), PCOL)
    reduced = jnp.sum(pieces, axis=0).reshape(16, 2, NB)

    result = -(placed[0] * reduced[None, :, 0] + placed[1] * reduced[None, :, 1])
    inv_panel = result.transpose(1, 0, 2).reshape(16, SIBS * NB)

    upper = result.reshape(SIBS, 16, 2, LANES).transpose(0, 2, 1, 3)
    upper = jnp.broadcast_to(upper[:, :, None], (SIBS, 2, 4, 16, LANES))
    upper = exchange(upper.reshape(NCOL, 16, LANES), PCOL).reshape(512, LANES)
    inv_upper = lax.dynamic_slice_in_dim(upper, col % 4 * 32, 32, 1).T

    term = jnp.dot(pair, upper, precision=HIGH, preferred_element_type=jnp.float32)
    term = term.reshape(2, 2, 16, LANES).transpose(1, 0, 2, 3).reshape(2, 32, LANES)
    term = exchange(to_all(term, 8).reshape(NROW, 32, LANES), PROW)
    term = jnp.sum(term, axis=0)
    mine = exchange(to_all(term, NCOL), PCOL)
    other = lax.ppermute(mine, "core", [(0, 1), (1, 0)])
    inv_diag = assemble(lax.axis_index("core").reshape(1), mine, other, diag_inv)
    return (inv_panel, inv_upper, inv_diag)


def solution(mesh):
    grid = Mesh(mesh.devices.reshape(2, 4, 2, 4, 4, 2), PROW + PCOL)
    placed = (P(PROW, PCOL), P(PROW, PCOL), P(), P(), P())
    return jax.shard_map(
        shards,
        mesh=grid,
        in_specs=placed,
        out_specs=(P(PROW + PCOL, None), P(PCOL, PROW), P()),
        check_vma=False,
    )
```

```python
import jax
import jax.numpy as jnp
from jax import lax
from jax.experimental import pallas as pl
from jax.experimental.pallas import tpu as pltpu
from jax.sharding import Mesh, PartitionSpec as P

NB = 256
SIBS = 4
PROW = ("zlo", "x", "core")
PCOL = ("zhi", "yhi", "ylo")
NROW = 16
NCOL = 32
LANES = 128
HIGH = lax.Precision.HIGH


def exchange(array, axes):
    return lax.all_to_all(array, axes, 0, 0, tiled=True)


def to_all(array, count):
    return jnp.broadcast_to(array[None], (count,) + array.shape)


def column_of_block():
    pairs = []
    for p in range(NROW):
        for s in range(SIBS):
            for c in range(8):
                source = p * NCOL + s * 8 + c
                target = (c * 2 + s // 2) * NCOL + 2 * p + s % 2
                pairs.append((source, target))
    return pairs


def assemble_kernel(core_ref, mine_ref, other_ref, diag_ref, out_ref):
    low_is_mine = core_ref[0] == 0
    for half in range(2):
        lanes = pl.ds(half * LANES, LANES)
        for part in range(4):
            for e in range(2):
                mine = mine_ref[half * 4 + part, pl.ds(e * 16, 16), :]
                other = other_ref[half * 4 + part, pl.ds(e * 16, 16), :]
                low = jnp.where(low_is_mine, mine, other)
                high = jnp.where(low_is_mine, other, mine)
                first = (e * 4 + part) * 32
                for rows, term in ((pl.ds(first, 16), low), (pl.ds(first + 16, 16), high)):
                    out_ref[0, rows, lanes] = diag_ref[0, rows, lanes] - term


def assemble(core, mine, other, diag_inv):
    pieces = pl.BlockSpec((8, 32, LANES), lambda s, core_ref: (s, 0, 0))
    block = pl.BlockSpec((1, NB, NB), lambda s, core_ref: (s, 0, 0))
    return pl.pallas_call(
        assemble_kernel,
        grid_spec=pltpu.PrefetchScalarGridSpec(
            num_scalar_prefetch=1,
            grid=(SIBS,),
            in_specs=[pieces, pieces, block],
            out_specs=block,
        ),
        out_shape=jax.ShapeDtypeStruct((SIBS, NB, NB), jnp.float32),
        compiler_params=pltpu.CompilerParams(vmem_limit_bytes=4 * 1024 * 1024),
    )(core, mine, other, diag_inv)


def shards(trailing, panels, diag_inv, ancestors, owner_map):
    row = lax.axis_index(PROW)
    col = lax.axis_index(PCOL)
    nblk = owner_map.shape[0]

    factor_t = panels.T
    moved = lax.ppermute(factor_t, PROW + PCOL, column_of_block())
    blocks = jnp.stack([col, 2 * row, 2 * row + 1, 2 * row + col // 16])
    number = jnp.sum(
        jnp.where(owner_map[None, :] == blocks[:, None], jnp.arange(nblk)[None, :], 0), axis=1
    )
    named = jnp.any(ancestors[None, :, :] == number[:, None, None], axis=2)
    sibling = jnp.arange(SIBS, dtype=jnp.int32)[None, :]
    first = jnp.min(jnp.where(named, sibling, SIBS), axis=1)
    last = jnp.max(jnp.where(named, sibling, -1), axis=1)
    slots = jnp.stack([first, last], axis=1)
    chosen = (slots[0][:, None] == sibling).reshape(8)
    matched = (slots[1:3].reshape(4)[:, None] == slots[0][None, :]).reshape(8)
    placed = (slots[3][:, None] == sibling).reshape(8)
    masks = jnp.concatenate([chosen, matched, placed]).astype(jnp.float32)
    masks = lax.optimization_barrier(jnp.broadcast_to(masks[:, None], (24, NB)))
    chosen = masks[0:8].reshape(2, SIBS, 1, NB)
    matched = masks[8:16].reshape(2, 2, 2, 1, 1, NB)
    placed = masks[16:24].reshape(2, SIBS, 1, NB)

    parts = moved.reshape(2, 16, 2, NB).transpose(0, 2, 1, 3).reshape(SIBS, 16, NB)
    parts = exchange(parts, ("core", "ylo"))
    parts = jnp.sum(chosen * parts[None], axis=1)
    parts, own = lax.optimization_barrier((parts, factor_t))
    block = exchange(to_all(parts.reshape(32, NB), NROW), PROW)
    across = lax.ppermute(own, "yhi", [(0, 2), (1, 3), (2, 0), (3, 1)])
    right = lax.axis_index("yhi") >= 2
    pair = jnp.concatenate(
        [jnp.where(right, across, own), jnp.where(right, own, across)]
    )
    block, pair = lax.optimization_barrier((block, pair))
    block = block.reshape(NROW, 2, 16, NB)

    sides = matched[:, :, 0] * block[None, None, :, 0] + matched[:, :, 1] * block[None, None, :, 1]
    sides = sides.reshape(2, 512, NB)
    product = lax.dot_general(
        trailing.reshape(2, NB, NB),
        sides,
        (((2,), (2,)), ((0,), (0,))),
        precision=HIGH,
        preferred_element_type=jnp.float32,
    )
    pieces = exchange(product.reshape(NCOL, 16, 512), PCOL)
    reduced = jnp.sum(pieces, axis=0).reshape(16, 2, NB)

    result = -(placed[0] * reduced[None, :, 0] + placed[1] * reduced[None, :, 1])
    inv_panel = result.transpose(1, 0, 2).reshape(16, SIBS * NB)

    upper = result.reshape(SIBS, 16, 2, LANES).transpose(0, 2, 1, 3)
    upper = jnp.broadcast_to(upper[:, :, None], (SIBS, 2, 4, 16, LANES))
    upper = exchange(upper.reshape(NCOL, 16, LANES), PCOL).reshape(512, LANES)
    inv_upper = lax.dynamic_slice_in_dim(upper, col % 4 * 32, 32, 1).T

    term = jnp.dot(pair, upper, precision=HIGH, preferred_element_type=jnp.float32)
    term = term.reshape(2, 2, 16, LANES).transpose(1, 0, 2, 3).reshape(2, 32, LANES)
    term = exchange(to_all(term, 8).reshape(NROW, 32, LANES), PROW)
    term = jnp.sum(term, axis=0)
    mine = exchange(to_all(term, NCOL), PCOL)
    other = lax.ppermute(mine, "core", [(0, 1), (1, 0)])
    inv_diag = assemble(lax.axis_index("core").reshape(1), mine, other, diag_inv)
    return (inv_panel, inv_upper, inv_diag)


def solution(mesh):
    grid = Mesh(mesh.devices.reshape(2, 4, 2, 4, 4, 2), PROW + PCOL)
    placed = (P(PROW, PCOL), P(PROW, PCOL), P(), P(), P())
    return jax.shard_map(
        shards,
        mesh=grid,
        in_specs=placed,
        out_specs=(P(PROW + PCOL, None), P(PCOL, PROW), P()),
        check_vma=False,
    )
```

```python
import jax
import jax.numpy as jnp
from jax import lax
from jax.experimental import pallas as pl
from jax.experimental.pallas import tpu as pltpu
from jax.sharding import Mesh, PartitionSpec as P

NB = 256
SIBS = 4
CHIP = ("zlo", "xh", "xl")
PROW = CHIP + ("core",)
PCOL = ("zhi", "yhi", "ylo")
NROW = 16
CHIPS = 8
NCOL = 32
LANES = 128
HIGH = lax.Precision.HIGH


def exchange(array, axes):
    return lax.all_to_all(array, axes, 0, 0, tiled=True)


def to_all(array, count):
    return jnp.broadcast_to(array[None], (count,) + array.shape)


def column_of_block():
    pairs = []
    for p in range(NROW):
        for s in range(SIBS):
            for c in range(8):
                source = p * NCOL + s * 8 + c
                chip = c % 4 * 2 + s // 2
                target = (chip * 2 + c // 4) * NCOL + 2 * p + s % 2
                pairs.append((source, target))
    return pairs


def assemble_kernel(core_ref, mine_ref, other_ref, diag_ref, out_ref):
    low_is_mine = core_ref[0] == 0
    for a in range(2):
        for c in range(2):
            tiles = []
            for b in range(2):
                part = a * 4 + b * 2 + c
                mine, other = mine_ref[part], other_ref[part]
                tiles.append(
                    (
                        jnp.where(low_is_mine, mine, other),
                        jnp.where(low_is_mine, other, mine),
                    )
                )
            for e in range(2):
                rows = pl.ds((a * 4 + e * 2 + c) * 32, 32)
                for half in range(2):
                    term = jnp.concatenate(
                        [tiles[b][half][:, e * 64 : e * 64 + 64] for b in range(2)], axis=1
                    )
                    lanes = pl.ds(half * LANES, LANES)
                    out_ref[0, rows, lanes] = diag_ref[0, rows, lanes] - term


def assemble(core, mine, other, diag_inv):
    pieces = pl.BlockSpec((8, 32, LANES), lambda s, core_ref: (s, 0, 0))
    block = pl.BlockSpec((1, NB, NB), lambda s, core_ref: (s, 0, 0))
    return pl.pallas_call(
        assemble_kernel,
        grid_spec=pltpu.PrefetchScalarGridSpec(
            num_scalar_prefetch=1,
            grid=(SIBS,),
            in_specs=[pieces, pieces, block],
            out_specs=block,
        ),
        out_shape=jax.ShapeDtypeStruct((SIBS, NB, NB), jnp.float32),
        compiler_params=pltpu.CompilerParams(vmem_limit_bytes=4 * 1024 * 1024),
    )(core, mine, other, diag_inv)


def swap_cores(array):
    return lax.ppermute(array, "core", [(0, 1), (1, 0)])


def shards(trailing, panels, diag_inv, ancestors, owner_map):
    row = lax.axis_index(PROW)
    col = lax.axis_index(PCOL)
    core = lax.axis_index("core")
    nblk = owner_map.shape[0]

    factor_t = panels.T
    moved = lax.ppermute(factor_t, PROW + PCOL, column_of_block())
    partner = swap_cores(trailing)

    beside = row + 1 - 2 * core
    half = col // 16
    blocks = jnp.stack(
        [
            col,
            2 * row,
            2 * row + 1,
            2 * beside,
            2 * beside + 1,
            2 * row + half,
            2 * beside + half,
        ]
    )
    number = jnp.sum(
        jnp.where(owner_map[None, :] == blocks[:, None], jnp.arange(nblk)[None, :], 0), axis=1
    )
    named = jnp.any(ancestors[None, :, :] == number[:, None, None], axis=2)
    sibling = jnp.arange(SIBS, dtype=jnp.int32)[None, :]
    first = jnp.min(jnp.where(named, sibling, SIBS), axis=1)
    last = jnp.max(jnp.where(named, sibling, -1), axis=1)
    slots = jnp.stack([first, last], axis=1)
    chosen = (slots[0][:, None] == sibling).reshape(8)
    matched = (slots[1:5].reshape(8)[:, None] == slots[0][None, :]).reshape(16)
    placed = (slots[5:7].reshape(4)[:, None] == sibling).reshape(16)
    masks = jnp.concatenate([chosen, matched, placed]).astype(jnp.float32)
    masks = lax.optimization_barrier(jnp.broadcast_to(masks[:, None], (40, NB)))
    chosen = masks[0:8].reshape(2, SIBS, 1, NB)
    matched = masks[8:24].reshape(4, 2, 2, 1, 1, NB)
    placed = masks[24:40, :LANES].reshape(2, 2, SIBS, 1, LANES)

    parts = moved.reshape(2, 16, 2, NB).transpose(0, 2, 1, 3).reshape(SIBS, 16, NB)
    parts = exchange(parts, ("xl", "ylo"))
    parts = jnp.sum(chosen * parts[None], axis=1)
    parts, own = lax.optimization_barrier((parts, factor_t))
    block = exchange(to_all(parts.reshape(32, NB), CHIPS), CHIP).reshape(CHIPS, 2, 16, NB)
    across = lax.ppermute(own, "yhi", [(0, 1), (1, 0), (2, 3), (3, 2)])
    right = lax.axis_index("yhi") % 2 == 1
    pair = jnp.concatenate([jnp.where(right, across, own), jnp.where(right, own, across)])

    sides = matched[:, :, 0] * block[None, None, :, 0] + matched[:, :, 1] * block[None, None, :, 1]
    sides = sides.reshape(2, 2, NB, NB)
    products = []
    for tile, side in ((trailing, sides[0]), (partner, sides[1])):
        product = lax.dot_general(
            tile.reshape(2, NB, NB),
            side,
            (((2,), (2,)), ((0,), (0,))),
            precision=HIGH,
            preferred_element_type=jnp.float32,
        )
        products.append(product.reshape(NCOL, 16, NB))
    pieces = exchange(jnp.stack(products, axis=1), PCOL)
    pair_beside = swap_cores(pair)
    pieces, pair, pair_beside = lax.optimization_barrier((pieces, pair, pair_beside))
    reduced = jnp.sum(pieces, axis=0)

    result = -(
        placed[:, 0] * reduced[:, None, :, :LANES] + placed[:, 1] * reduced[:, None, :, LANES:]
    )

    upper = result.reshape(2, SIBS, 16, 2, 64).transpose(1, 3, 2, 0, 4)
    upper = upper.reshape(SIBS, 1, 2, 1, 16, LANES)
    upper = jnp.broadcast_to(upper, (SIBS, 2, 2, 2, 16, LANES)).reshape(NCOL, 16, LANES)
    upper = exchange(upper, PCOL).reshape(512, LANES)

    term = jnp.dot(
        pair, upper[:, :64], precision=HIGH, preferred_element_type=jnp.float32
    ) + jnp.dot(
        pair_beside, upper[:, 64:], precision=HIGH, preferred_element_type=jnp.float32
    )
    term = jnp.concatenate([term[:32], term[32:]], axis=1)
    term = jnp.sum(exchange(to_all(term, CHIPS), CHIP), axis=0)
    mine = exchange(to_all(term, NCOL), PCOL)
    got = swap_cores(result[1])
    low = jnp.where(core == 0, result[0], got)
    high = jnp.where(core == 0, got, result[0])
    inv_panel = jnp.stack([low, high], axis=1).transpose(2, 0, 1, 3).reshape(16, SIBS * NB)
    odd = lax.axis_index("ylo") == 1
    keep = jnp.where(odd, upper[:, 32:64], upper[:, :32]).T
    give = jnp.where(odd, upper[:, 96:], upper[:, 64:96]).T
    inv_upper = jnp.where(lax.axis_index("yhi") // 2 == core, keep, swap_cores(give))
    mine, inv_upper, inv_panel = lax.optimization_barrier((mine, inv_upper, inv_panel))
    other = swap_cores(mine)
    inv_diag = assemble(core.reshape(1), mine, other, diag_inv)

    return (inv_panel, inv_upper, inv_diag)


def solution(mesh):
    grid = Mesh(mesh.devices.reshape(2, 2, 2, 2, 4, 4, 2), PROW + PCOL)
    placed = (P(PROW, PCOL), P(PROW, PCOL), P(), P(), P())
    return jax.shard_map(
        shards,
        mesh=grid,
        in_specs=placed,
        out_specs=(P(PROW + PCOL, None), P(PCOL, PROW), P()),
        check_vma=False,
    )
```

```python
import jax
import jax.numpy as jnp
from jax import lax
from jax.experimental import pallas as pl
from jax.experimental.pallas import tpu as pltpu
from jax.sharding import Mesh, PartitionSpec as P

NB = 256
SIBS = 4
CHIP = ("zlo", "xh", "xl")
PROW = CHIP + ("core",)
PCOL = ("zhi", "yhi", "ylo")
NROW = 16
CHIPS = 8
NCOL = 32
LANES = 128
HIGH = lax.Precision.HIGH


def exchange(array, axes):
    return lax.all_to_all(array, axes, 0, 0, tiled=True)


def to_all(array, count):
    return jnp.broadcast_to(array[None], (count,) + array.shape)


def column_of_block():
    pairs = []
    for p in range(NROW):
        for s in range(SIBS):
            for c in range(8):
                source = p * NCOL + s * 8 + c
                chip = c % 4 * 2 + s // 2
                target = (chip * 2 + c // 4) * NCOL + 2 * p + s % 2
                pairs.append((source, target))
    return pairs


def assemble_kernel(core_ref, mine_ref, other_ref, diag_ref, out_ref):
    low_is_mine = core_ref[0] == 0
    for a in range(2):
        for c in range(2):
            tiles = []
            for b in range(2):
                part = a * 4 + b * 2 + c
                mine, other = mine_ref[part], other_ref[part]
                tiles.append(
                    (
                        jnp.where(low_is_mine, mine, other),
                        jnp.where(low_is_mine, other, mine),
                    )
                )
            for e in range(2):
                rows = pl.ds((a * 4 + e * 2 + c) * 32, 32)
                for half in range(2):
                    term = jnp.concatenate(
                        [tiles[b][half][:, e * 64 : e * 64 + 64] for b in range(2)], axis=1
                    )
                    lanes = pl.ds(half * LANES, LANES)
                    out_ref[0, rows, lanes] = diag_ref[0, rows, lanes] - term


def assemble(core, mine, other, diag_inv):
    pieces = pl.BlockSpec((8, 32, LANES), lambda s, core_ref: (s, 0, 0))
    block = pl.BlockSpec((1, NB, NB), lambda s, core_ref: (s, 0, 0))
    return pl.pallas_call(
        assemble_kernel,
        grid_spec=pltpu.PrefetchScalarGridSpec(
            num_scalar_prefetch=1,
            grid=(SIBS,),
            in_specs=[pieces, pieces, block],
            out_specs=block,
        ),
        out_shape=jax.ShapeDtypeStruct((SIBS, NB, NB), jnp.float32),
        compiler_params=pltpu.CompilerParams(vmem_limit_bytes=4 * 1024 * 1024),
    )(core, mine, other, diag_inv)


def swap_cores(array):
    return lax.ppermute(array, "core", [(0, 1), (1, 0)])


def shards(trailing, panels, diag_inv, ancestors, owner_map):
    row = lax.axis_index(PROW)
    col = lax.axis_index(PCOL)
    core = lax.axis_index("core")
    nblk = owner_map.shape[0]

    factor_t = panels.T
    moved = lax.ppermute(factor_t, PROW + PCOL, column_of_block())
    partner = swap_cores(trailing)

    beside = row + 1 - 2 * core
    half = col // 16
    blocks = jnp.stack(
        [
            col,
            2 * row,
            2 * row + 1,
            2 * beside,
            2 * beside + 1,
            2 * row + half,
            2 * beside + half,
        ]
    )
    number = jnp.sum(
        jnp.where(owner_map[None, :] == blocks[:, None], jnp.arange(nblk)[None, :], 0), axis=1
    )
    named = jnp.any(ancestors[None, :, :] == number[:, None, None], axis=2)
    sibling = jnp.arange(SIBS, dtype=jnp.int32)[None, :]
    first = jnp.min(jnp.where(named, sibling, SIBS), axis=1)
    last = jnp.max(jnp.where(named, sibling, -1), axis=1)
    slots = jnp.stack([first, last], axis=1)
    held = jnp.any(slots[0][:, None] == sibling, axis=0)
    matched = ((slots[1:5].reshape(8)[:, None] == sibling) & held[None, :]).reshape(32)
    placed = (slots[5:7].reshape(4)[:, None] == sibling).reshape(16)
    masks = jnp.concatenate([matched, placed]).astype(jnp.float32)
    masks = lax.optimization_barrier(jnp.broadcast_to(masks[:, None], (48, NB)))
    matched = masks[0:32].reshape(4, 2, SIBS, 1, 1, NB)
    placed = masks[32:48, :LANES].reshape(2, 2, SIBS, 1, LANES)

    halves = moved.reshape(32, 2, NB).transpose(1, 0, 2)
    halves, own = lax.optimization_barrier((halves, factor_t))
    halves = to_all(halves, CHIPS)
    block = exchange(halves.reshape(NROW, 32, NB), CHIP + ("ylo",)).reshape(4, SIBS, 32, NB)
    across = lax.ppermute(own, "yhi", [(0, 1), (1, 0), (2, 3), (3, 2)])
    right = lax.axis_index("yhi") % 2 == 1
    pair = jnp.concatenate([jnp.where(right, across, own), jnp.where(right, own, across)])

    sides = sum(matched[:, :, s] * block[None, None, :, s] for s in range(SIBS))
    sides = sides.reshape(2, 2, NB, NB)
    products = []
    for tile, side in ((trailing, sides[0]), (partner, sides[1])):
        product = lax.dot_general(
            tile.reshape(2, NB, NB),
            side,
            (((2,), (2,)), ((0,), (0,))),
            precision=HIGH,
            preferred_element_type=jnp.float32,
        )
        products.append(product.reshape(NCOL, 16, NB))
    pieces = exchange(jnp.stack(products, axis=1), PCOL)
    pair_beside = swap_cores(pair)
    pieces, pair, pair_beside = lax.optimization_barrier((pieces, pair, pair_beside))
    reduced = jnp.sum(pieces, axis=0)

    result = -(
        placed[:, 0] * reduced[:, None, :, :LANES] + placed[:, 1] * reduced[:, None, :, LANES:]
    )

    upper = result.reshape(2, SIBS, 16, 2, 64).transpose(1, 3, 2, 0, 4)
    upper = upper.reshape(SIBS, 1, 2, 1, 16, LANES)
    upper = jnp.broadcast_to(upper, (SIBS, 2, 2, 2, 16, LANES)).reshape(NCOL, 16, LANES)
    upper = exchange(upper, PCOL).reshape(512, LANES)

    term = jnp.dot(
        pair, upper[:, :64], precision=HIGH, preferred_element_type=jnp.float32
    ) + jnp.dot(
        pair_beside, upper[:, 64:], precision=HIGH, preferred_element_type=jnp.float32
    )
    term = jnp.concatenate([term[:32], term[32:]], axis=1)
    term = jnp.sum(exchange(to_all(term, CHIPS), CHIP), axis=0)
    mine = exchange(to_all(term, NCOL), PCOL)
    got = swap_cores(result[1])
    low = jnp.where(core == 0, result[0], got)
    high = jnp.where(core == 0, got, result[0])
    inv_panel = jnp.stack([low, high], axis=1).transpose(2, 0, 1, 3).reshape(16, SIBS * NB)
    odd = lax.axis_index("ylo") == 1
    keep = jnp.where(odd, upper[:, 32:64], upper[:, :32]).T
    give = jnp.where(odd, upper[:, 96:], upper[:, 64:96]).T
    inv_upper = jnp.where(lax.axis_index("yhi") // 2 == core, keep, swap_cores(give))
    mine, inv_upper, inv_panel = lax.optimization_barrier((mine, inv_upper, inv_panel))
    other = swap_cores(mine)
    inv_diag = assemble(core.reshape(1), mine, other, diag_inv)

    return (inv_panel, inv_upper, inv_diag)


def solution(mesh):
    grid = Mesh(mesh.devices.reshape(2, 2, 2, 2, 4, 4, 2), PROW + PCOL)
    placed = (P(PROW, PCOL), P(PROW, PCOL), P(), P(), P())
    return jax.shard_map(
        shards,
        mesh=grid,
        in_specs=placed,
        out_specs=(P(PROW + PCOL, None), P(PCOL, PROW), P()),
        check_vma=False,
    )
```

```python
import jax
import jax.numpy as jnp
from jax import lax
from jax.experimental import pallas as pl
from jax.experimental.pallas import tpu as pltpu
from jax.sharding import Mesh, PartitionSpec as P

NB = 256
SIBS = 4
CHIP = ("zlo", "xh", "xl")
PROW = CHIP + ("core",)
PCOL = ("zhi", "yhi", "ylo")
NROW = 16
CHIPS = 8
NCOL = 32
LANES = 128
HIGH = lax.Precision.HIGH


def exchange(array, axes):
    return lax.all_to_all(array, axes, 0, 0, tiled=True)


def to_all(array, count):
    return jnp.broadcast_to(array[None], (count,) + array.shape)


def column_of_block():
    pairs = []
    for p in range(NROW):
        for s in range(SIBS):
            for c in range(8):
                source = p * NCOL + s * 8 + c
                chip = c % 4 * 2 + s // 2
                target = (chip * 2 + c // 4) * NCOL + 2 * p + s % 2
                pairs.append((source, target))
    return pairs


def assemble_kernel(core_ref, mine_ref, other_ref, diag_ref, out_ref):
    low_is_mine = core_ref[0] == 0
    sibling = pl.program_id(0)
    for a in range(2):
        for c in range(2):
            tiles = []
            for b in range(2):
                part = sibling * 8 + a * 4 + b * 2 + c
                mine, other = mine_ref[part], other_ref[part]
                tiles.append(
                    (
                        jnp.where(low_is_mine, mine, other),
                        jnp.where(low_is_mine, other, mine),
                    )
                )
            for e in range(2):
                rows = pl.ds((a * 4 + e * 2 + c) * 32, 32)
                for half in range(2):
                    term = jnp.concatenate(
                        [tiles[b][half][:, e * 64 : e * 64 + 64] for b in range(2)], axis=1
                    )
                    lanes = pl.ds(half * LANES, LANES)
                    out_ref[0, rows, lanes] = diag_ref[sibling, rows, lanes] - term


def assemble(core, mine, other, diag_inv):
    whole = pl.BlockSpec(memory_space=pltpu.VMEM)
    block = pl.BlockSpec((1, NB, NB), lambda s, core_ref: (s, 0, 0))
    return pl.pallas_call(
        assemble_kernel,
        grid_spec=pltpu.PrefetchScalarGridSpec(
            num_scalar_prefetch=1,
            grid=(SIBS,),
            in_specs=[whole, whole, whole],
            out_specs=block,
        ),
        out_shape=jax.ShapeDtypeStruct((SIBS, NB, NB), jnp.float32),
        compiler_params=pltpu.CompilerParams(vmem_limit_bytes=4 * 1024 * 1024),
    )(core, mine, other, diag_inv)


def swap_cores(array):
    return lax.ppermute(array, "core", [(0, 1), (1, 0)])


def shards(trailing, panels, diag_inv, ancestors, owner_map):
    row = lax.axis_index(PROW)
    col = lax.axis_index(PCOL)
    core = lax.axis_index("core")
    nblk = owner_map.shape[0]

    factor_t = panels.T
    moved = lax.ppermute(factor_t, PROW + PCOL, column_of_block())
    odd = lax.axis_index("ylo") == 1
    chunks = trailing.reshape(NROW, 2, 16, NB)
    keep = jnp.where(odd, chunks[:, 1], chunks[:, 0])
    give = jnp.where(odd, chunks[:, 0], chunks[:, 1])
    lent = lax.ppermute(give, "ylo", [(0, 1), (1, 0)])
    tiles = jnp.stack([jnp.where(odd, lent, keep), jnp.where(odd, keep, lent)])
    partner = swap_cores(tiles)

    beside = row + 1 - 2 * core
    half = col // 16
    blocks = jnp.stack(
        [
            col // 2 * 2,
            col // 2 * 2 + 1,
            2 * row,
            2 * row + 1,
            2 * beside,
            2 * beside + 1,
            2 * row + half,
            2 * beside + half,
        ]
    )
    number = jnp.sum(
        jnp.where(owner_map[None, :] == blocks[:, None], jnp.arange(nblk)[None, :], 0), axis=1
    )
    named = jnp.any(ancestors[None, :, :] == number[:, None, None], axis=2)
    sibling = jnp.arange(SIBS, dtype=jnp.int32)[None, :]
    first = jnp.min(jnp.where(named, sibling, SIBS), axis=1)
    last = jnp.max(jnp.where(named, sibling, -1), axis=1)
    slots = jnp.stack([first, last], axis=1)
    held = jnp.any(slots[0:2][:, :, None] == sibling[None], axis=1)
    matched = slots[2:6].reshape(1, 8, 1) == sibling[None]
    matched = (matched & held[:, None, :]).reshape(64)
    placed = (slots[6:8].reshape(4)[:, None] == sibling).reshape(16)
    masks = jnp.concatenate([matched, placed]).astype(jnp.float32)
    masks = lax.optimization_barrier(jnp.broadcast_to(masks[:, None], (80, NB)))
    matched = masks[0:64].reshape(2, 4, 2, SIBS, 1, 1, NB)
    placed = masks[64:80, :LANES].reshape(2, 2, SIBS, 1, LANES)

    moved, own = lax.optimization_barrier((moved, factor_t))
    block = to_all(moved, NROW)
    block = exchange(block, CHIP + ("ylo",)).reshape(4, SIBS, 32, 512)
    across = lax.ppermute(own, "yhi", [(0, 1), (1, 0), (2, 3), (3, 2)])
    right = lax.axis_index("yhi") % 2 == 1
    pair = jnp.concatenate([jnp.where(right, across, own), jnp.where(right, own, across)])

    sides = []
    for k in range(2):
        rows = block[:, :, :, k * NB : (k + 1) * NB]
        side = sum(matched[k][:, :, s] * rows[None, None, :, s] for s in range(SIBS))
        sides.append(side.reshape(2, 2, NB, NB))
    products = []
    for r, part in ((0, tiles), (1, partner)):
        product = 0.0
        for k in range(2):
            product += lax.dot_general(
                part[k].reshape(2, LANES, NB),
                sides[k][r],
                (((2,), (2,)), ((0,), (0,))),
                precision=HIGH,
                preferred_element_type=jnp.float32,
            )
        products.append(product.reshape(NROW, 16, NB))
    pieces = exchange(jnp.stack(products, axis=1), ("zhi", "yhi"))
    pair_beside = swap_cores(pair)
    pieces, pair, pair_beside = lax.optimization_barrier((pieces, pair, pair_beside))
    reduced = jnp.sum(pieces, axis=0)

    result = -(
        placed[:, 0] * reduced[:, None, :, :LANES] + placed[:, 1] * reduced[:, None, :, LANES:]
    )

    upper = result.reshape(2, SIBS, 16, 2, 64).transpose(1, 3, 2, 0, 4)
    upper = upper.reshape(SIBS, 1, 2, 1, 16, LANES)
    upper = jnp.broadcast_to(upper, (SIBS, 2, 2, 2, 16, LANES)).reshape(NCOL, 16, LANES)
    upper = exchange(upper, PCOL).reshape(512, LANES)

    term = jnp.dot(
        pair, upper[:, :64], precision=HIGH, preferred_element_type=jnp.float32
    ) + jnp.dot(
        pair_beside, upper[:, 64:], precision=HIGH, preferred_element_type=jnp.float32
    )
    term = jnp.concatenate([term[:32], term[32:]], axis=1)
    term = jnp.sum(exchange(to_all(term, CHIPS), CHIP), axis=0)
    mine = exchange(to_all(term, NCOL), PCOL)
    got = swap_cores(result[1])
    low = jnp.where(core == 0, result[0], got)
    high = jnp.where(core == 0, got, result[0])
    inv_panel = jnp.stack([low, high], axis=1).transpose(2, 0, 1, 3).reshape(16, SIBS * NB)
    keep = jnp.where(odd, upper[:, 32:64], upper[:, :32]).T
    give = jnp.where(odd, upper[:, 96:], upper[:, 64:96]).T
    inv_upper = jnp.where(lax.axis_index("yhi") // 2 == core, keep, swap_cores(give))
    mine, inv_upper, inv_panel = lax.optimization_barrier((mine, inv_upper, inv_panel))
    other = swap_cores(mine)
    inv_diag = assemble(core.reshape(1), mine, other, diag_inv)

    return (inv_panel, inv_upper, inv_diag)


def solution(mesh):
    grid = Mesh(mesh.devices.reshape(2, 2, 2, 2, 4, 4, 2), PROW + PCOL)
    placed = (P(PROW, PCOL), P(PROW, PCOL), P(), P(), P())
    return jax.shard_map(
        shards,
        mesh=grid,
        in_specs=placed,
        out_specs=(P(PROW + PCOL, None), P(PCOL, PROW), P()),
        check_vma=False,
    )
```

```python
import jax
import jax.numpy as jnp
from jax import lax
from jax.experimental import pallas as pl
from jax.experimental.pallas import tpu as pltpu
from jax.sharding import Mesh, PartitionSpec as P

NB = 256
SIBS = 4
CHIP = ("zlo", "xh", "xl")
PROW = CHIP + ("core",)
PCOL = ("zhi", "yhi", "ylo")
NROW = 16
CHIPS = 8
NCOL = 32
LANES = 128
HIGH = lax.Precision.HIGH


def exchange(array, axes):
    return lax.all_to_all(array, axes, 0, 0, tiled=True)


def to_all(array, count):
    return jnp.broadcast_to(array[None], (count,) + array.shape)


def column_of_block():
    pairs = []
    for p in range(NROW):
        for s in range(SIBS):
            for c in range(8):
                source = p * NCOL + s * 8 + c
                chip = c % 4 * 2 + s // 2
                target = (chip * 2 + c // 4) * NCOL + 2 * p + s % 2
                pairs.append((source, target))
    return pairs


def assemble_kernel(core_ref, mine_ref, other_ref, diag_ref, out_ref):
    low_is_mine = core_ref[0] == 0
    for a in range(2):
        for c in range(2):
            tiles = []
            for b in range(2):
                part = a * 4 + b * 2 + c
                mine, other = mine_ref[part], other_ref[part]
                tiles.append(
                    (
                        jnp.where(low_is_mine, mine, other),
                        jnp.where(low_is_mine, other, mine),
                    )
                )
            for e in range(2):
                rows = pl.ds((a * 4 + e * 2 + c) * 32, 32)
                for half in range(2):
                    term = jnp.concatenate(
                        [tiles[b][half][:, e * 64 : e * 64 + 64] for b in range(2)], axis=1
                    )
                    lanes = pl.ds(half * LANES, LANES)
                    out_ref[0, rows, lanes] = diag_ref[0, rows, lanes] - term


def assemble(core, mine, other, diag_inv):
    pieces = pl.BlockSpec((8, 32, LANES), lambda s, core_ref: (s, 0, 0))
    block = pl.BlockSpec((1, NB, NB), lambda s, core_ref: (s, 0, 0))
    return pl.pallas_call(
        assemble_kernel,
        grid_spec=pltpu.PrefetchScalarGridSpec(
            num_scalar_prefetch=1,
            grid=(SIBS,),
            in_specs=[pieces, pieces, block],
            out_specs=block,
        ),
        out_shape=jax.ShapeDtypeStruct((SIBS, NB, NB), jnp.float32),
        compiler_params=pltpu.CompilerParams(vmem_limit_bytes=4 * 1024 * 1024),
    )(core, mine, other, diag_inv)


def swap_cores(array):
    return lax.ppermute(array, "core", [(0, 1), (1, 0)])


def shards(trailing, panels, diag_inv, ancestors, owner_map):
    row = lax.axis_index(PROW)
    col = lax.axis_index(PCOL)
    core = lax.axis_index("core")
    nblk = owner_map.shape[0]

    factor_t = panels.T
    moved = lax.ppermute(factor_t, PROW + PCOL, column_of_block())
    odd = lax.axis_index("ylo") == 1
    chunks = trailing.reshape(NROW, 2, 16, NB)
    keep = jnp.where(odd, chunks[:, 1], chunks[:, 0])
    give = jnp.where(odd, chunks[:, 0], chunks[:, 1])
    lent = lax.ppermute(give, "ylo", [(0, 1), (1, 0)])
    tiles = jnp.stack([jnp.where(odd, lent, keep), jnp.where(odd, keep, lent)])
    partner = swap_cores(tiles)

    beside = row + 1 - 2 * core
    half = col // 16
    blocks = jnp.stack(
        [
            col // 2 * 2,
            col // 2 * 2 + 1,
            2 * row,
            2 * row + 1,
            2 * beside,
            2 * beside + 1,
            2 * row + half,
            2 * beside + half,
        ]
    )
    number = jnp.sum(
        jnp.where(owner_map[None, :] == blocks[:, None], jnp.arange(nblk)[None, :], 0), axis=1
    )
    named = jnp.any(ancestors[None, :, :] == number[:, None, None], axis=2)
    sibling = jnp.arange(SIBS, dtype=jnp.int32)[None, :]
    first = jnp.min(jnp.where(named, sibling, SIBS), axis=1)
    last = jnp.max(jnp.where(named, sibling, -1), axis=1)
    slots = jnp.stack([first, last], axis=1)
    held = jnp.any(slots[0:2][:, :, None] == sibling[None], axis=1)
    matched = slots[2:6].reshape(1, 8, 1) == sibling[None]
    matched = (matched & held[:, None, :]).reshape(64)
    placed = (slots[6:8].reshape(4)[:, None] == sibling).reshape(16)
    masks = jnp.concatenate([matched, placed]).astype(jnp.float32)
    masks = lax.optimization_barrier(jnp.broadcast_to(masks[:, None], (80, NB)))
    matched = masks[0:64].reshape(2, 4, 2, SIBS, 1, 1, NB)
    placed = masks[64:80, :LANES].reshape(2, 2, SIBS, 1, LANES)

    own = factor_t
    block = to_all(moved, NROW)
    block = exchange(block, CHIP + ("ylo",)).reshape(4, SIBS, 32, 512)
    across = lax.ppermute(own, "yhi", [(0, 1), (1, 0), (2, 3), (3, 2)])
    right = lax.axis_index("yhi") % 2 == 1
    pair = jnp.concatenate([jnp.where(right, across, own), jnp.where(right, own, across)])

    sides = []
    for k in range(2):
        rows = block[:, :, :, k * NB : (k + 1) * NB]
        side = sum(matched[k][:, :, s] * rows[None, None, :, s] for s in range(SIBS))
        sides.append(side.reshape(2, 2, NB, NB))
    products = []
    for r, part in ((0, tiles), (1, partner)):
        product = 0.0
        for k in range(2):
            product += lax.dot_general(
                part[k].reshape(2, LANES, NB),
                sides[k][r],
                (((2,), (2,)), ((0,), (0,))),
                precision=HIGH,
                preferred_element_type=jnp.float32,
            )
        products.append(product.reshape(NROW, 16, NB))
    pieces = exchange(jnp.stack(products, axis=1), ("zhi", "yhi"))
    pair_beside = swap_cores(pair)
    pieces, pair, pair_beside = lax.optimization_barrier((pieces, pair, pair_beside))
    reduced = jnp.sum(pieces, axis=0)

    result = -(
        placed[:, 0] * reduced[:, None, :, :LANES] + placed[:, 1] * reduced[:, None, :, LANES:]
    )

    upper = result.reshape(2, SIBS, 16, 2, 64).transpose(1, 3, 2, 0, 4)
    upper = upper.reshape(SIBS, 1, 2, 1, 16, LANES)
    upper = jnp.broadcast_to(upper, (SIBS, 2, 2, 2, 16, LANES)).reshape(NCOL, 16, LANES)
    upper = exchange(upper, PCOL).reshape(512, LANES)

    term = jnp.dot(
        pair, upper[:, :64], precision=HIGH, preferred_element_type=jnp.float32
    ) + jnp.dot(
        pair_beside, upper[:, 64:], precision=HIGH, preferred_element_type=jnp.float32
    )
    term = jnp.concatenate([term[:32], term[32:]], axis=1)
    term = jnp.sum(exchange(to_all(term, CHIPS), CHIP), axis=0)
    mine = exchange(to_all(term, NCOL), PCOL)
    got = swap_cores(result[1])
    low = jnp.where(core == 0, result[0], got)
    high = jnp.where(core == 0, got, result[0])
    inv_panel = jnp.stack([low, high], axis=1).transpose(2, 0, 1, 3).reshape(16, SIBS * NB)
    keep = jnp.where(odd, upper[:, 32:64], upper[:, :32]).T
    give = jnp.where(odd, upper[:, 96:], upper[:, 64:96]).T
    inv_upper = jnp.where(lax.axis_index("yhi") // 2 == core, keep, swap_cores(give))
    mine, inv_upper, inv_panel = lax.optimization_barrier((mine, inv_upper, inv_panel))
    other = swap_cores(mine)
    inv_diag = assemble(core.reshape(1), mine, other, diag_inv)

    return (inv_panel, inv_upper, inv_diag)


def solution(mesh):
    grid = Mesh(mesh.devices.reshape(2, 2, 2, 2, 4, 4, 2), PROW + PCOL)
    placed = (P(PROW, PCOL), P(PROW, PCOL), P(), P(), P())
    return jax.shard_map(
        shards,
        mesh=grid,
        in_specs=placed,
        out_specs=(P(PROW + PCOL, None), P(PCOL, PROW), P()),
        check_vma=False,
    )
```
